32 devices in a mesh: groups: 2 (over y), seq: 4 (over z), head: 4 (over x, core).
Axes of the slice: x: 2, y: 2, z: 4, core: 2. Of those that a mesh axis runs over, the one named last changes fastest.
Arguments:
- x_in: bfloat16 [1024, 8192], P(('groups', 'seq'), 'head'), parts along dimension 0, may hold values from -6 to 6
- bc_in: bfloat16 [1024, 8, 256], P(('groups', 'seq'), 'head'), parts along dimension 0, may hold values from -6 to 6
- z_in: bfloat16 [1024, 8192], P(('groups', 'seq'), 'head'), parts along dimension 0, may hold values from -6 to 6
- dt_raw: float32 [1024, 128], P(('groups', 'seq'), 'head'), parts along dimension 0, may hold values from -12 to 0
- conv_x: float32 [4, 8192], P(None, 'head'), may hold values from -3 to 3
- conv_bc: float32 [4, 8, 256], P(None, 'head'), may hold values from -3 to 3
- a_log: float32 [128], P('head'), may hold values from -0.35 to 0.35
- d_skip: float32 [128], P('head'), may hold values from 0.5 to 1.5
- norm_gain: float32 [8192], P('head'), may hold values from 0.25 to 1.75
Outputs:
- out: bfloat16 [1024, 8192], P(('groups', 'seq'), 'head'), parts along dimension 0
The draws below stay inside these ranges and needn't reach their ends.
There are 2 independent parts, one for each index of `groups`. The reference program is written for one: setup_inputs(seed, part) draws one part's arguments, and reference() takes and returns one part's arrays. A program takes and returns all parts, laid end to end along the dimension named above; an argument that names none is the same for every part. Nothing has to cross between parts.
All inputs are finite; a program needn't handle non-finite values.
Results may differ from the reference program's by a relative error of at most 0.0056.
Values may be sent and summed in bfloat16 or wider, within the bound.
A program may use at most 192 MiB of HBM per device.

```python
import jax
import jax.numpy as jnp
from jax import lax

LOCAL_HEADS = 128
HEAD_DIM = 64
STATE = 128
BC_GROUPS = 8
CONV = 4
BLOCK = 128
WINDOW_TOKENS = 512
INNER = 8192


def draw_dt_raw(key, part):
    random_keys = jax.random.split(key, 6)
    share = 0.5
    slow = jax.random.uniform(random_keys[0], (LOCAL_HEADS,)) < share
    fast_rate = 1.0 / jax.random.uniform(random_keys[1], (LOCAL_HEADS,), minval=30.0, maxval=50.0)
    slow_rate = jax.random.uniform(random_keys[2], (LOCAL_HEADS,), minval=0.25, maxval=0.5) / WINDOW_TOKENS
    baseline_rate = jnp.where(slow, slow_rate, fast_rate)
    noisy_steps = jnp.exp(jax.random.uniform(random_keys[3], (WINDOW_TOKENS, LOCAL_HEADS), minval=-0.5, maxval=0.5))
    spike_positions = jax.random.randint(random_keys[4], (3,), 0, WINDOW_TOKENS)
    spike_draw = jnp.any(jnp.arange(WINDOW_TOKENS)[:, None] == spike_positions[None, :], axis=1)
    spike_height = jax.random.uniform(random_keys[5], (WINDOW_TOKENS, LOCAL_HEADS), minval=0.25, maxval=0.5)
    time_step_values = jnp.where(spike_draw[:, None], spike_height, baseline_rate[None, :] * noisy_steps)
    return jnp.log(jnp.expm1(time_step_values)).astype(jnp.float32)


def block_levels(stream_key, extent, pieces, smallest, largest):
    def one(axis_at, blocks):
        draws = jax.random.uniform(jax.random.fold_in(jax.random.fold_in(stream_key, 6), axis_at), (blocks,), jnp.float32, smallest / len(pieces), largest / len(pieces))
        return jnp.repeat(jnp.exp(draws), extent[axis_at] // blocks).reshape((-1,) + (1,) * (len(extent) - axis_at - 1))

    level = one(*pieces[0])
    for cut in pieces[1:]:
        level = level * one(*cut)
    return level


def bell_draw(rng, shape, spread, most, cuts=(), dtype=jnp.bfloat16):
    drawn = spread * jax.random.normal(rng, shape, jnp.float32)
    if cuts:
        drawn = drawn * block_levels(rng, shape, cuts, -0.22, 0.18)
    return jnp.clip(drawn, -most, most).astype(dtype)


def setup_inputs(seed: int = 0, part: int = 0) -> dict:
    arg_keys = jax.random.split(jax.random.key(seed), 10)
    part_keys = jax.random.split(jax.random.fold_in(arg_keys[9], part), 10)
    x_in = bell_draw(part_keys[0], (WINDOW_TOKENS, INNER), 1.0, 6.0, ((0, 4), (1, 4)))
    bc_in = bell_draw(part_keys[1], (WINDOW_TOKENS, BC_GROUPS, 2 * STATE), 1.0, 6.0, ((0, 4), (1, 4)))
    z_in = bell_draw(part_keys[2], (WINDOW_TOKENS, INNER), 1.0, 6.0, ((0, 4), (1, 4)))
    dt_raw = draw_dt_raw(jax.random.fold_in(jax.random.fold_in(arg_keys[9], part), 71), part)
    conv_x = bell_draw(arg_keys[4], (CONV, INNER), CONV ** -0.5, 3.0, ((1, 4),), jnp.float32)
    conv_bc = bell_draw(arg_keys[5], (CONV, BC_GROUPS, 2 * STATE), CONV ** -0.5, 3.0, ((1, 4),), jnp.float32)
    a_log = jnp.clip(jax.random.uniform(arg_keys[6], (LOCAL_HEADS,), jnp.float32, -0.35, 0.35) * block_levels(arg_keys[6], (LOCAL_HEADS,), ((0, 4),), -0.4, 0.0), -0.35, 0.35)
    d_skip = jnp.clip(0.5 + 1.0 * jax.random.uniform(arg_keys[7], (LOCAL_HEADS,), jnp.float32) ** block_levels(arg_keys[7], (LOCAL_HEADS,), ((0, 4),), -0.2, 0.2), 0.5, 1.5)
    norm_gain = jnp.clip(1.0 + 0.15 * jax.random.normal(arg_keys[8], (INNER,), jnp.float32), 0.25, 1.75)
    return {"x_in": x_in, "bc_in": bc_in, "z_in": z_in, "dt_raw": dt_raw, "conv_x": conv_x, "conv_bc": conv_bc, "a_log": a_log, "d_skip": d_skip, "norm_gain": norm_gain}


EPS = 1e-05

def conv_silu(tail_rows, series, taps):
    length = series.shape[0]
    padded = jnp.concatenate([tail_rows, series.astype(jnp.float32)], axis=0)
    running = jnp.zeros(series.shape, jnp.float32)
    for offset in range(taps.shape[0]):
        running = running + taps[offset] * padded[offset:offset + length]
    return jax.nn.silu(running).astype(jnp.bfloat16)

def block_terms(inputs, b_input, c_output, deltas, rates):
    cum_rate = jnp.cumsum(rates, axis=0)
    cum_moved = jnp.transpose(cum_rate, (1, 2, 0))
    delta_moved = jnp.transpose(deltas, (1, 2, 0))
    places = jnp.arange(cum_rate.shape[0])
    causal = places[:, None] >= places[None, :]
    gaps_all = cum_moved[..., :, None] - cum_moved[..., None, :]
    decays = jnp.where(causal, jnp.exp(jnp.where(causal, gaps_all, 0.0)), 0.0)
    intersection = jnp.einsum('tgn,sgn->gts', c_output.astype(jnp.float32), b_input.astype(jnp.float32))
    weight = (decays * delta_moved[..., None, :] * intersection[:, None]).astype(jnp.bfloat16)
    y_intra = jnp.einsum('ghts,sghp->tghp', weight.astype(jnp.float32), inputs.astype(jnp.float32))
    tail_decay = jnp.exp(cum_rate[-1] - cum_rate) * deltas
    scaled = (tail_decay[..., None] * inputs.astype(jnp.float32)).astype(jnp.bfloat16)
    states = jnp.einsum('sghp,sgn->ghpn', scaled.astype(jnp.float32), b_input.astype(jnp.float32))
    return (y_intra, states, cum_rate, jnp.exp(cum_rate[-1]))

def block_output(y_intra, cum_rate, c_output, inputs, gates, incoming, skip, gain):
    state_half = incoming.astype(jnp.bfloat16)
    from_state = jnp.einsum('tgn,ghpn->tghp', c_output.astype(jnp.float32), state_half.astype(jnp.float32))
    mixed = y_intra + jnp.exp(cum_rate)[..., None] * from_state + skip[..., None] * inputs.astype(jnp.float32)
    gated = mixed * jax.nn.silu(gates.astype(jnp.float32))
    mean_sq = lax.optimization_barrier(jnp.mean(gated * gated, axis=(2, 3), keepdims=True))
    return (gated * lax.rsqrt(mean_sq + EPS) * gain).astype(jnp.bfloat16)

def reference(x_in, bc_in, z_in, dt_raw, conv_x, conv_bc, a_log, d_skip, norm_gain):
    rim = CONV - 1
    x_act = conv_silu(jnp.zeros((rim, INNER), jnp.float32), x_in, conv_x)
    bc_act = conv_silu(jnp.zeros((rim, BC_GROUPS, 2 * STATE), jnp.float32), bc_in, conv_bc)
    deltas = jax.nn.softplus(dt_raw)
    rates = -jnp.exp(a_log)[None, :] * deltas
    per_group = LOCAL_HEADS // BC_GROUPS
    block_count = WINDOW_TOKENS // BLOCK
    inputs = x_act.reshape(block_count, BLOCK, BC_GROUPS, per_group, HEAD_DIM)
    b_input = bc_act[:, :, :STATE].reshape(block_count, BLOCK, BC_GROUPS, STATE)
    c_output = bc_act[:, :, STATE:].reshape(block_count, BLOCK, BC_GROUPS, STATE)
    delta_blocks = deltas.reshape(block_count, BLOCK, BC_GROUPS, per_group)
    rate_blocks = rates.reshape(block_count, BLOCK, BC_GROUPS, per_group)
    gates = z_in.reshape(block_count, BLOCK, BC_GROUPS, per_group, HEAD_DIM)
    skip = d_skip.reshape(BC_GROUPS, per_group)
    gain = norm_gain.reshape(BC_GROUPS, per_group, HEAD_DIM)

    def advance(carry, piece):
        inputs_b, b_part, c_part, delta_part, rate_part, gate_part = piece
        y_intra, states, cum_rate, block_decay = block_terms(inputs_b, b_part, c_part, delta_part, rate_part)
        result = block_output(y_intra, cum_rate, c_part, inputs_b, gate_part, carry, skip, gain)
        return (block_decay[..., None, None] * carry + states, result)
    start = jnp.zeros((BC_GROUPS, per_group, HEAD_DIM, STATE), jnp.float32)
    _, outputs = lax.scan(advance, start, (inputs, b_input, c_output, delta_blocks, rate_blocks, gates))
    return outputs.reshape(WINDOW_TOKENS, INNER)
```

```python
import functools

import jax
import jax.numpy as jnp
from jax import lax
from jax.experimental import pallas as pl
from jax.experimental.pallas import tpu as pltpu
from jax.sharding import PartitionSpec as P

BLOCK = 128
EPS = 1e-05
HALO = 16
HEADS_PER_CHUNK = 4
F32 = jnp.float32
BF16 = jnp.bfloat16
MESH = pl.DeviceIdType.MESH


def silu(v):
    half = 0.5 * v
    return half + half * jnp.tanh(half)


def kernel(
    n, groups, heads, x_ref, bc_ref, z_ref, dt_ref, cx_ref, cbc_ref, al_ref, ds_ref, gain_ref,
    o_ref, xh, bh, sendb, recvb, own, gated, ec, xs, bs, xact, cum_t, dt_t, col_cum, col_tail,
    pad, inter, c_act, b_t, h_send, h_recv, s_send, s_recv,
):
    tokens, width = x_ref.shape
    head_dim = width // heads
    per_chunk = xact.shape[2] // head_dim
    wide = xact.shape[2]
    chunks = width // wide
    group_chunks = chunks // groups
    state = bc_ref.shape[1] // groups // 2
    taps = cx_ref.shape[0]
    base = 8 - (taps - 1)
    me = lax.axis_index("seq")

    def halo_copies():
        rows = pl.ds(tokens - HALO, HALO)
        return [
            pltpu.make_async_remote_copy(
                src_ref=src.at[rows], dst_ref=dst, send_sem=h_send.at[i], recv_sem=h_recv.at[i],
                device_id={"seq": me + 1}, device_id_type=MESH,
            )
            for i, (src, dst) in enumerate(((bc_ref, bh), (x_ref, xh)))
        ]

    def state_copy(k):
        return pltpu.make_async_remote_copy(
            src_ref=sendb.at[k], dst_ref=recvb.at[k], send_sem=s_send.at[k],
            recv_sem=s_recv.at[k], device_id={"seq": me + 1}, device_id_type=MESH,
        )

    barrier = pltpu.get_barrier_semaphore()

    @pl.when(me > 0)
    def _():
        pl.semaphore_signal(barrier, inc=1, device_id={"seq": me - 1}, device_id_type=MESH)

    @pl.when(me < n - 1)
    def _():
        pl.semaphore_wait(barrier, 1)
        for copy in halo_copies():
            copy.start()

    row = lax.broadcasted_iota(jnp.int32, (tokens, tokens), 0)
    col = lax.broadcasted_iota(jnp.int32, (tokens, tokens), 1)
    causal = row >= col
    raw = dt_ref[...]
    deltas = jnp.maximum(raw, 0.0) + jnp.log1p(jnp.exp(-jnp.abs(raw)))
    rates = -jnp.exp(al_ref[...]) * deltas
    cum = jnp.dot(
        causal.astype(F32), rates, precision=lax.Precision.HIGHEST, preferred_element_type=F32
    )
    tail = jnp.exp(cum[tokens - 1 : tokens] - cum) * deltas
    for k in range(chunks):
        part = slice(k * per_chunk, (k + 1) * per_chunk)
        col_cum[k] = cum[:, part]
        col_tail[k] = tail[:, part]
    pad[...] = jnp.zeros_like(pad)
    pad[:, :heads] = cum
    cum_t[...] = pad[...].T[:heads]
    pad[:, :heads] = deltas
    dt_t[...] = pad[...].T[:heads]

    @pl.when(me == 0)
    def _():
        xh[...] = jnp.zeros_like(xh)
        bh[...] = jnp.zeros_like(bh)

    @pl.when(me > 0)
    def _():
        for copy in halo_copies():
            copy.wait_recv()

    bs[0:8] = bh[...].astype(F32)[HALO - 8 :]
    bs[8:] = bc_ref[...].astype(F32)
    for g in range(groups):
        span = slice(g * 2 * state, (g + 1) * 2 * state)
        total = cbc_ref[0, g : g + 1, :] * bs[base : base + tokens, span]
        for k in range(1, taps):
            total = total + cbc_ref[k, g : g + 1, :] * bs[base + k : base + k + tokens, span]
        act = silu(total)
        b_part = act[:, :state].astype(BF16)
        c_part = act[:, state:].astype(BF16)
        c_act[g] = c_part
        b_t[g] = b_part.astype(F32).T.astype(BF16)
        product = lax.dot_general(
            c_part, b_part, (((1,), (1,)), ((), ())), preferred_element_type=F32
        )
        inter[g] = jnp.where(causal, product, 0.0)

    head_of_lane = lax.broadcasted_iota(jnp.int32, (tokens, wide), 1) // head_dim

    def spread(columns):
        result = jnp.broadcast_to(columns[:, per_chunk - 1 :], (tokens, wide))
        for h in range(per_chunk - 2, -1, -1):
            result = jnp.where(head_of_lane == h, columns[:, h : h + 1], result)
        return result

    def make_state(k, carry):
        g = k // group_chunks
        cols = pl.ds(pl.multiple_of(k * wide, wide), wide)
        xs[0:8] = xh[:, cols].astype(F32)[HALO - 8 :]
        xs[8:] = x_ref[:, cols].astype(F32)
        weights = cx_ref[:, cols]
        total = weights[0:1] * xs[base : base + tokens]
        for i in range(1, taps):
            total = total + weights[i : i + 1] * xs[base + i : base + i + tokens]
        act = silu(total).astype(BF16)
        xact[k] = act
        ec[k] = jnp.exp(spread(col_cum[k]))
        scaled = (spread(col_tail[k]) * act.astype(F32)).astype(BF16)
        made = jnp.dot(b_t[g], scaled, preferred_element_type=F32)
        own[k] = made

        @pl.when((me == 0) & (me < n - 1))
        def _():
            sendb[k] = made.astype(BF16)
            state_copy(k).start()

        return carry

    lax.fori_loop(0, chunks, make_state, 0)

    def group_step(g, carry):
        def chunk_step(j, squares):
            k = g * group_chunks + j
            cols = pl.ds(pl.multiple_of(k * wide, wide), wide)

            @pl.when(me > 0)
            def _():
                state_copy(k).wait_recv()

            @pl.when((me > 0) & (me < n - 1))
            def _():
                decay = ec[k, tokens - 1 : tokens, :]
                sendb[k] = (decay * recvb[k].astype(F32) + own[k]).astype(BF16)
                state_copy(k).start()

            act = xact[k]
            columns = col_cum[k]
            parts = []
            skips = jnp.zeros((1, wide), F32)
            for h in range(per_chunk):
                at = k * per_chunk + h
                gap = jnp.minimum(columns[:, h : h + 1] - cum_t[pl.ds(at, 1), :], 0.0)
                weight = (jnp.exp(gap) * dt_t[pl.ds(at, 1), :] * inter[g]).astype(BF16)
                parts.append(
                    jnp.dot(
                        weight, act[:, h * head_dim : (h + 1) * head_dim],
                        preferred_element_type=F32,
                    )
                )
                skips = jnp.where(head_of_lane[0:1] == h, ds_ref[at], skips)
            gated[k] = jnp.concatenate(parts, axis=1) + skips * act.astype(F32)

            @pl.when(me > 0)
            def _():
                gated[k] += ec[k] * jnp.dot(c_act[g], recvb[k], preferred_element_type=F32)

            done = gated[k] * silu(z_ref[:, cols].astype(F32))
            gated[k] = done
            return squares + jnp.sum(done * done, axis=1, keepdims=True)

        squares = lax.fori_loop(0, group_chunks, chunk_step, jnp.zeros((tokens, 1), F32))
        scale = lax.rsqrt(squares * (groups / width) + EPS)

        def finish(j, carry):
            k = g * group_chunks + j
            cols = pl.ds(pl.multiple_of(k * wide, wide), wide)
            o_ref[:, cols] = (gated[k] * scale * gain_ref[:, cols]).astype(BF16)
            return carry

        return lax.fori_loop(0, group_chunks, finish, carry)

    lax.fori_loop(0, groups, group_step, 0)

    @pl.when(me < n - 1)
    def _():
        for copy in halo_copies():
            copy.wait_send()

        def drain(k, carry):
            state_copy(k).wait_send()
            return carry

        lax.fori_loop(0, chunks, drain, 0)


def shards(x_in, bc_in, z_in, dt_raw, conv_x, conv_bc, a_log, d_skip, norm_gain):
    tokens, width = x_in.shape
    assert tokens == BLOCK
    groups = bc_in.shape[1]
    heads = dt_raw.shape[1]
    state = bc_in.shape[2] // 2
    head_dim = width // heads
    per_chunk = min(HEADS_PER_CHUNK, heads // groups)
    wide = per_chunk * head_dim
    chunks = width // wide
    n = lax.axis_size("seq")
    vmem = pl.BlockSpec(memory_space=pltpu.VMEM)
    smem = pl.BlockSpec(memory_space=pltpu.SMEM)
    V = pltpu.VMEM
    dma = pltpu.SemaphoreType.DMA
    return pl.pallas_call(
        functools.partial(kernel, n, groups, heads),
        out_shape=jax.ShapeDtypeStruct((tokens, width), BF16),
        in_specs=[vmem] * 7 + [smem, vmem],
        out_specs=vmem,
        scratch_shapes=[
            V((HALO, width), BF16),
            V((HALO, groups * 2 * state), BF16),
            V((chunks, state, wide), BF16),
            V((chunks, state, wide), BF16),
            V((chunks, state, wide), F32),
            V((chunks, tokens, wide), F32),
            V((chunks, tokens, wide), F32),
            V((tokens + 8, wide), F32),
            V((tokens + 8, groups * 2 * state), F32),
            V((chunks, tokens, wide), BF16),
            V((heads, tokens), F32),
            V((heads, tokens), F32),
            V((chunks, tokens, per_chunk), F32),
            V((chunks, tokens, per_chunk), F32),
            V((tokens, 128), F32),
            V((groups, tokens, tokens), F32),
            V((groups, tokens, state), BF16),
            V((groups, state, tokens), BF16),
            dma((2,)),
            dma((2,)),
            dma((chunks,)),
            dma((chunks,)),
        ],
        compiler_params=pltpu.CompilerParams(
            collective_id=0, has_side_effects=True, vmem_limit_bytes=40 * 1024 * 1024
        ),
    )(
        x_in, bc_in.reshape(tokens, groups * 2 * state), z_in, dt_raw, conv_x, conv_bc,
        a_log.reshape(1, heads), d_skip, norm_gain.reshape(1, width),
    )


def solution(mesh):
    return jax.shard_map(
        shards,
        mesh=mesh,
        in_specs=(
            P(("groups", "seq"), "head"),
            P(("groups", "seq"), "head", None),
            P(("groups", "seq"), "head"),
            P(("groups", "seq"), "head"),
            P(None, "head"),
            P(None, "head", None),
            P("head"),
            P("head"),
            P("head"),
        ),
        out_specs=P(("groups", "seq"), "head"),
        check_vma=False,
    )
```

```python
import functools

import jax
import jax.numpy as jnp
from jax import lax
from jax.experimental import pallas as pl
from jax.experimental.pallas import tpu as pltpu
from jax.sharding import PartitionSpec as P

BLOCK = 128
EPS = 1e-05
HALO = 16
LIMIT = 66400000
HEADS_PER_CHUNK = 4
F32 = jnp.float32
BF16 = jnp.bfloat16
MESH = pl.DeviceIdType.MESH


def silu(v):
    half = 0.5 * v
    return half + half * jnp.tanh(half)


def kernel(
    n, groups, heads, x_hbm, bc_hbm, z_hbm, dt_hbm, cx_hbm, cbc_hbm, al_hbm, ds_hbm, gain_hbm,
    o_ref, x_ref, bc_ref, z_ref, dt_ref, cx_ref, cbc_ref, al_ref, ds_ref, gain_ref, xh, bh, sendb, recvb, own, gated, ec, xs, bs, xact, cum_t, dt_t, col_cum, col_tail,
    pad, square, inter, c_act, b_t, h_send, h_recv, s_send, s_recv, x_sem, z_sem, p_sem,
):
    tokens, width = x_hbm.shape
    head_dim = width // heads
    per_chunk = xact.shape[2] // head_dim
    wide = xact.shape[2]
    chunks = width // wide
    group_chunks = chunks // groups
    state = bc_hbm.shape[1] // groups // 2
    taps = cx_ref.shape[0]
    base = 8 - (taps - 1)
    me = lax.axis_index("seq")

    def halo_copies():
        rows = pl.ds(tokens - HALO, HALO)
        return [
            pltpu.make_async_remote_copy(
                src_ref=src.at[rows], dst_ref=dst, send_sem=h_send.at[i], recv_sem=h_recv.at[i],
                device_id={"seq": me + 1}, device_id_type=MESH,
            )
            for i, (src, dst) in enumerate(((bc_hbm, bh), (x_hbm, xh)))
        ]

    def state_copy(k):
        return pltpu.make_async_remote_copy(
            src_ref=sendb.at[k], dst_ref=recvb.at[k], send_sem=s_send.at[k],
            recv_sem=s_recv.at[k], device_id={"seq": me + 1}, device_id_type=MESH,
        )

    def columns_of(k):
        return pl.ds(pl.multiple_of(k * wide, wide), wide)

    def x_copy(k):
        return pltpu.make_async_copy(x_hbm.at[:, columns_of(k)], x_ref.at[k], x_sem.at[k])

    def z_copy(k):
        return pltpu.make_async_copy(z_hbm.at[:, columns_of(k)], z_ref.at[k], z_sem.at[k])

    pairs = (
        (dt_hbm, dt_ref), (al_hbm, al_ref), (cbc_hbm, cbc_ref), (cx_hbm, cx_ref),
        (ds_hbm, ds_ref), (gain_hbm, gain_ref), (bc_hbm, bc_ref),
    )
    small = [pltpu.make_async_copy(a, b, p_sem.at[i]) for i, (a, b) in enumerate(pairs)]

    barrier = pltpu.get_barrier_semaphore()

    @pl.when(me > 0)
    def _():
        pl.semaphore_signal(barrier, inc=1, device_id={"seq": me - 1}, device_id_type=MESH)

    for copy in small:
        copy.start()

    def fetch_x(k, carry):
        x_copy(k).start()
        return carry

    def fetch_z(k, carry):
        z_copy(k).start()
        return carry

    lax.fori_loop(0, chunks, fetch_x, 0)
    lax.fori_loop(0, chunks, fetch_z, 0)

    @pl.when(me < n - 1)
    def _():
        pl.semaphore_wait(barrier, 1)
        for copy in halo_copies():
            copy.start()

    row = lax.broadcasted_iota(jnp.int32, (tokens, tokens), 0)
    col = lax.broadcasted_iota(jnp.int32, (tokens, tokens), 1)
    causal = row >= col
    small[0].wait()
    small[1].wait()
    raw = dt_ref[...]
    softplus = jnp.maximum(raw, 0.0) + jnp.log1p(jnp.exp(-jnp.abs(raw)))
    dt_t[...] = softplus
    pad[...] = jnp.zeros_like(pad)
    pad[:heads] = softplus
    deltas = pad[...].T[:, :heads]
    rates = -jnp.exp(al_ref[...]) * deltas
    cum = jnp.dot(
        causal.astype(F32), rates, precision=lax.Precision.HIGHEST, preferred_element_type=F32
    )
    tail = jnp.exp(cum[tokens - 1 : tokens] - cum) * deltas
    for k in range(chunks):
        part = slice(k * per_chunk, (k + 1) * per_chunk)
        col_cum[k] = cum[:, part]
        col_tail[k] = tail[:, part]
    square[...] = jnp.zeros_like(square)
    square[:, :heads] = cum
    cum_t[...] = square[...].T[:heads]

    @pl.when(me == 0)
    def _():
        xh[...] = jnp.zeros_like(xh)
        bh[...] = jnp.zeros_like(bh)

    @pl.when(me > 0)
    def _():
        for copy in halo_copies():
            copy.wait_recv()

    small[2].wait()
    small[6].wait()
    bs[0:8] = bh[...].astype(F32)[HALO - 8 :]
    bs[8:] = bc_ref[...].astype(F32)
    for g in range(groups):
        span = slice(g * 2 * state, (g + 1) * 2 * state)
        total = cbc_ref[0, g : g + 1, :] * bs[base : base + tokens, span]
        for k in range(1, taps):
            total = total + cbc_ref[k, g : g + 1, :] * bs[base + k : base + k + tokens, span]
        act = silu(total)
        b_part = act[:, :state].astype(BF16)
        c_part = act[:, state:].astype(BF16)
        c_act[g] = c_part
        b_t[g] = b_part.astype(F32).T.astype(BF16)
        product = lax.dot_general(
            c_part, b_part, (((1,), (1,)), ((), ())), preferred_element_type=F32
        )
        inter[g] = jnp.where(causal, product, 0.0)

    head_of_lane = lax.broadcasted_iota(jnp.int32, (tokens, wide), 1) // head_dim

    def spread(columns):
        result = jnp.broadcast_to(columns[:, per_chunk - 1 :], (tokens, wide))
        for h in range(per_chunk - 2, -1, -1):
            result = jnp.where(head_of_lane == h, columns[:, h : h + 1], result)
        return result

    for copy in small[3:6]:
        copy.wait()

    def make_state(k, carry):
        g = k // group_chunks
        cols = columns_of(k)
        x_copy(k).wait()
        xs[0:8] = xh[:, cols].astype(F32)[HALO - 8 :]
        xs[8:] = x_ref[k].astype(F32)
        weights = cx_ref[:, cols]
        total = weights[0:1] * xs[base : base + tokens]
        for i in range(1, taps):
            total = total + weights[i : i + 1] * xs[base + i : base + i + tokens]
        act = silu(total).astype(BF16)
        xact[k] = act
        ec[k] = jnp.exp(spread(col_cum[k]))
        scaled = (spread(col_tail[k]) * act.astype(F32)).astype(BF16)
        made = jnp.dot(b_t[g], scaled, preferred_element_type=F32)
        own[k] = made

        @pl.when((me == 0) & (me < n - 1))
        def _():
            sendb[k] = made.astype(BF16)
            state_copy(k).start()

        return carry

    lax.fori_loop(0, chunks, make_state, 0)

    def group_step(g, carry):
        def chunk_step(j, squares):
            k = g * group_chunks + j
            act = xact[k]
            columns = col_cum[k]
            parts = []
            skips = jnp.zeros((1, wide), F32)
            for h in range(per_chunk):
                at = k * per_chunk + h
                gap = jnp.minimum(columns[:, h : h + 1] - cum_t[pl.ds(at, 1), :], 0.0)
                weight = (jnp.exp(gap) * dt_t[pl.ds(at, 1), :] * inter[g]).astype(BF16)
                parts.append(
                    jnp.dot(
                        weight, act[:, h * head_dim : (h + 1) * head_dim],
                        preferred_element_type=F32,
                    )
                )
                skips = jnp.where(head_of_lane[0:1] == h, ds_ref[at], skips)
            gated[k] = jnp.concatenate(parts, axis=1) + skips * act.astype(F32)

            z_copy(k).wait()
            gate = silu(z_ref[k].astype(F32))

            @pl.when(me > 0)
            def _():
                state_copy(k).wait_recv()

            @pl.when((me > 0) & (me < n - 1))
            def _():
                decay = ec[k, tokens - 1 : tokens, :]
                sendb[k] = (decay * recvb[k].astype(F32) + own[k]).astype(BF16)
                state_copy(k).start()

            @pl.when(me > 0)
            def _():
                gated[k] += ec[k] * jnp.dot(c_act[g], recvb[k], preferred_element_type=F32)

            done = gated[k] * gate
            gated[k] = done
            return squares + jnp.sum(done * done, axis=1, keepdims=True)

        squares = lax.fori_loop(0, group_chunks, chunk_step, jnp.zeros((tokens, 1), F32))
        scale = lax.rsqrt(squares * (groups / width) + EPS)

        def finish(j, carry):
            k = g * group_chunks + j
            cols = columns_of(k)
            o_ref[:, cols] = (gated[k] * scale * gain_ref[:, cols]).astype(BF16)
            return carry

        return lax.fori_loop(0, group_chunks, finish, carry)

    lax.fori_loop(0, groups, group_step, 0)

    @pl.when(me < n - 1)
    def _():
        for copy in halo_copies():
            copy.wait_send()

        def drain(k, carry):
            state_copy(k).wait_send()
            return carry

        lax.fori_loop(0, chunks, drain, 0)


def shards(x_in, bc_in, z_in, dt_raw, conv_x, conv_bc, a_log, d_skip, norm_gain):
    tokens, width = x_in.shape
    assert tokens == BLOCK
    groups = bc_in.shape[1]
    heads = dt_raw.shape[1]
    state = bc_in.shape[2] // 2
    head_dim = width // heads
    per_chunk = min(HEADS_PER_CHUNK, heads // groups)
    wide = per_chunk * head_dim
    chunks = width // wide
    n = lax.axis_size("seq")
    vmem = pl.BlockSpec(memory_space=pltpu.VMEM)
    hbm = pl.BlockSpec(memory_space=pltpu.HBM)
    V = pltpu.VMEM
    dma = pltpu.SemaphoreType.DMA
    return pl.pallas_call(
        functools.partial(kernel, n, groups, heads),
        out_shape=jax.ShapeDtypeStruct((tokens, width), BF16),
        in_specs=[hbm] * 9,
        out_specs=vmem,
        scratch_shapes=[
            V((chunks, tokens, wide), BF16),
            V((tokens, groups * 2 * state), BF16),
            V((chunks, tokens, wide), BF16),
            V((heads, tokens), F32),
            V(conv_x.shape, F32),
            V(conv_bc.shape, F32),
            V((1, heads), F32),
            pltpu.SMEM((heads,), F32),
            V((1, width), F32),
            V((HALO, width), BF16),
            V((HALO, groups * 2 * state), BF16),
            V((chunks, state, wide), BF16),
            V((chunks, state, wide), BF16),
            V((chunks, state, wide), F32),
            V((chunks, tokens, wide), F32),
            V((chunks, tokens, wide), F32),
            V((tokens + 8, wide), F32),
            V((tokens + 8, groups * 2 * state), F32),
            V((chunks, tokens, wide), BF16),
            V((heads, tokens), F32),
            V((heads, tokens), F32),
            V((chunks, tokens, per_chunk), F32),
            V((chunks, tokens, per_chunk), F32),
            V((128, tokens), F32),
            V((tokens, 128), F32),
            V((groups, tokens, tokens), F32),
            V((groups, tokens, state), BF16),
            V((groups, state, tokens), BF16),
            dma((2,)),
            dma((2,)),
            dma((chunks,)),
            dma((chunks,)),
            dma((chunks,)),
            dma((chunks,)),
            dma((7,)),
        ],
        compiler_params=pltpu.CompilerParams(
            collective_id=0, has_side_effects=True, vmem_limit_bytes=LIMIT
        ),
    )(
        x_in, bc_in.reshape(tokens, groups * 2 * state), z_in, dt_raw.T, conv_x, conv_bc,
        a_log.reshape(1, heads), d_skip, norm_gain.reshape(1, width),
    )


def solution(mesh):
    return jax.shard_map(
        shards,
        mesh=mesh,
        in_specs=(
            P(("groups", "seq"), "head"),
            P(("groups", "seq"), "head", None),
            P(("groups", "seq"), "head"),
            P(("groups", "seq"), "head"),
            P(None, "head"),
            P(None, "head", None),
            P("head"),
            P("head"),
            P("head"),
        ),
        out_specs=P(("groups", "seq"), "head"),
        check_vma=False,
    )
```

```python
import functools

import jax
import jax.numpy as jnp
from jax import lax
from jax.experimental import pallas as pl
from jax.experimental.pallas import tpu as pltpu
from jax.sharding import PartitionSpec as P

BLOCK = 128
EPS = 1e-05
HALO = 16
LIMIT = 55000000
HEADS_PER_CHUNK = 4
F32 = jnp.float32
BF16 = jnp.bfloat16
MESH = pl.DeviceIdType.MESH


def silu(v):
    half = 0.5 * v
    return half + half * jnp.tanh(half)


def kernel(
    n, groups, heads, x_hbm, bc_hbm, z_hbm, dt_hbm, cx_hbm, cbc_hbm, al_hbm, ds_hbm, gain_hbm,
    o_ref, x_ref, bc_ref, z_ref, dt_ref, cx_ref, cbc_ref, al_ref, ds_ref, gain_ref, xh, bh, sendb, recvb, own, gated, ec, xs, bs, xact, cum_t, dt_t, col_cum, col_tail,
    pad, square, inter, c_act, b_t, h_send, h_recv, s_send, s_recv, x_sem, z_sem, p_sem,
):
    tokens, width = x_hbm.shape
    head_dim = width // heads
    per_chunk = xact.shape[2] // head_dim
    wide = xact.shape[2]
    chunks = width // wide
    group_chunks = chunks // groups
    state = bc_hbm.shape[1] // groups // 2
    taps = cx_ref.shape[0]
    base = 8 - (taps - 1)
    me = lax.axis_index("seq")

    def halo_copies():
        rows = pl.ds(tokens - HALO, HALO)
        return [
            pltpu.make_async_remote_copy(
                src_ref=src.at[rows], dst_ref=dst, send_sem=h_send.at[i], recv_sem=h_recv.at[i],
                device_id={"seq": me + 1}, device_id_type=MESH,
            )
            for i, (src, dst) in enumerate(((bc_hbm, bh), (x_hbm, xh)))
        ]

    def state_copy(k):
        return pltpu.make_async_remote_copy(
            src_ref=sendb.at[k], dst_ref=recvb.at[k], send_sem=s_send.at[k],
            recv_sem=s_recv.at[k], device_id={"seq": me + 1}, device_id_type=MESH,
        )

    def columns_of(k):
        return pl.ds(pl.multiple_of(k * wide, wide), wide)

    def x_copy(k):
        return pltpu.make_async_copy(x_hbm.at[:, columns_of(k)], x_ref.at[k], x_sem.at[k])

    def z_copy(k):
        return pltpu.make_async_copy(z_hbm.at[:, columns_of(k)], z_ref.at[k], z_sem.at[k])

    pairs = (
        (dt_hbm, dt_ref), (al_hbm, al_ref), (cbc_hbm, cbc_ref), (cx_hbm, cx_ref),
        (ds_hbm, ds_ref), (gain_hbm, gain_ref), (bc_hbm, bc_ref),
    )
    small = [pltpu.make_async_copy(a, b, p_sem.at[i]) for i, (a, b) in enumerate(pairs)]

    barrier = pltpu.get_barrier_semaphore()

    @pl.when(me > 0)
    def _():
        pl.semaphore_signal(barrier, inc=1, device_id={"seq": me - 1}, device_id_type=MESH)

    for copy in small:
        copy.start()

    def fetch_x(k, carry):
        x_copy(k).start()
        return carry

    def fetch_z(k, carry):
        z_copy(k).start()
        return carry

    lax.fori_loop(0, chunks, fetch_x, 0)

    @pl.when(me < n - 1)
    def _():
        pl.semaphore_wait(barrier, 1)
        for copy in halo_copies():
            copy.start()

    row = lax.broadcasted_iota(jnp.int32, (tokens, tokens), 0)
    col = lax.broadcasted_iota(jnp.int32, (tokens, tokens), 1)
    causal = row >= col
    small[0].wait()
    small[1].wait()
    raw = dt_ref[...]
    softplus = jnp.maximum(raw, 0.0) + jnp.log1p(jnp.exp(-jnp.abs(raw)))
    dt_t[...] = softplus
    pad[...] = jnp.zeros_like(pad)
    pad[:heads] = softplus
    deltas = pad[...].T[:, :heads]
    rates = -jnp.exp(al_ref[...]) * deltas
    cum = jnp.dot(
        causal.astype(F32), rates, precision=lax.Precision.HIGHEST, preferred_element_type=F32
    )
    tail = jnp.exp(cum[tokens - 1 : tokens] - cum) * deltas
    for k in range(chunks):
        part = slice(k * per_chunk, (k + 1) * per_chunk)
        col_cum[k] = cum[:, part]
        col_tail[k] = tail[:, part]
    square[...] = jnp.zeros_like(square)
    square[:, :heads] = cum
    cum_t[...] = square[...].T[:heads]

    lax.fori_loop(0, chunks, fetch_z, 0)

    @pl.when(me == 0)
    def _():
        xh[...] = jnp.zeros_like(xh)
        bh[...] = jnp.zeros_like(bh)

    @pl.when(me > 0)
    def _():
        for copy in halo_copies():
            copy.wait_recv()

    small[2].wait()
    small[6].wait()
    bs[0:8] = bh[...].astype(F32)[HALO - 8 :]
    bs[8:] = bc_ref[...].astype(F32)
    for g in range(groups):
        span = slice(g * 2 * state, (g + 1) * 2 * state)
        total = cbc_ref[0, g : g + 1, :] * bs[base : base + tokens, span]
        for k in range(1, taps):
            total = total + cbc_ref[k, g : g + 1, :] * bs[base + k : base + k + tokens, span]
        act = silu(total)
        b_part = act[:, :state].astype(BF16)
        c_part = act[:, state:].astype(BF16)
        c_act[g] = c_part
        b_t[g] = b_part.astype(F32).T.astype(BF16)
        product = lax.dot_general(
            c_part, b_part, (((1,), (1,)), ((), ())), preferred_element_type=F32
        )
        inter[g] = jnp.where(causal, product, 0.0)

    head_of_lane = lax.broadcasted_iota(jnp.int32, (tokens, wide), 1) // head_dim

    def spread(columns):
        result = jnp.broadcast_to(columns[:, per_chunk - 1 :], (tokens, wide))
        for h in range(per_chunk - 2, -1, -1):
            result = jnp.where(head_of_lane == h, columns[:, h : h + 1], result)
        return result

    for copy in small[3:6]:
        copy.wait()

    def make_state(g, k):
        cols = columns_of(k)
        x_copy(k).wait()
        xs[0:8] = xh[:, cols].astype(F32)[HALO - 8 :]
        xs[8:] = x_ref[k].astype(F32)
        weights = cx_ref[:, cols]
        total = weights[0:1] * xs[base : base + tokens]
        for i in range(1, taps):
            total = total + weights[i : i + 1] * xs[base + i : base + i + tokens]
        act = silu(total).astype(BF16)
        xact[k] = act
        ec[k] = jnp.exp(spread(col_cum[k]))
        scaled = (spread(col_tail[k]) * act.astype(F32)).astype(BF16)
        made = jnp.dot(b_t[g], scaled, preferred_element_type=F32)
        own[k] = made

        @pl.when((me == 0) & (me < n - 1))
        def _():
            sendb[k] = made.astype(BF16)
            state_copy(k).start()


    def group_step(g, carry):
        def chunk_step(j, squares):
            k = g * group_chunks + j
            make_state(g, k)
            act = xact[k]
            columns = col_cum[k]
            parts = []
            skips = jnp.zeros((1, wide), F32)
            for h in range(per_chunk):
                at = k * per_chunk + h
                gap = jnp.minimum(columns[:, h : h + 1] - cum_t[pl.ds(at, 1), :], 0.0)
                weight = (jnp.exp(gap) * dt_t[pl.ds(at, 1), :] * inter[g]).astype(BF16)
                parts.append(
                    jnp.dot(
                        weight, act[:, h * head_dim : (h + 1) * head_dim],
                        preferred_element_type=F32,
                    )
                )
                skips = jnp.where(head_of_lane[0:1] == h, ds_ref[at], skips)
            gated[k] = jnp.concatenate(parts, axis=1) + skips * act.astype(F32)

            z_copy(k).wait()
            gate = silu(z_ref[k].astype(F32))

            @pl.when(me > 0)
            def _():
                state_copy(k).wait_recv()

            @pl.when((me > 0) & (me < n - 1))
            def _():
                decay = ec[k, tokens - 1 : tokens, :]
                sendb[k] = (decay * recvb[k].astype(F32) + own[k]).astype(BF16)
                state_copy(k).start()

            @pl.when(me > 0)
            def _():
                gated[k] += ec[k] * jnp.dot(c_act[g], recvb[k], preferred_element_type=F32)

            done = gated[k] * gate
            gated[k] = done
            return squares + jnp.sum(done * done, axis=1, keepdims=True)

        squares = lax.fori_loop(0, group_chunks, chunk_step, jnp.zeros((tokens, 1), F32))
        scale = lax.rsqrt(squares * (groups / width) + EPS)

        def finish(j, carry):
            k = g * group_chunks + j
            cols = columns_of(k)
            o_ref[:, cols] = (gated[k] * scale * gain_ref[:, cols]).astype(BF16)
            return carry

        return lax.fori_loop(0, group_chunks, finish, carry)

    lax.fori_loop(0, groups, group_step, 0)

    @pl.when(me < n - 1)
    def _():
        for copy in halo_copies():
            copy.wait_send()

        def drain(k, carry):
            state_copy(k).wait_send()
            return carry

        lax.fori_loop(0, chunks, drain, 0)


def shards(x_in, bc_in, z_in, dt_raw, conv_x, conv_bc, a_log, d_skip, norm_gain):
    tokens, width = x_in.shape
    assert tokens == BLOCK
    groups = bc_in.shape[1]
    heads = dt_raw.shape[1]
    state = bc_in.shape[2] // 2
    head_dim = width // heads
    per_chunk = min(HEADS_PER_CHUNK, heads // groups)
    wide = per_chunk * head_dim
    chunks = width // wide
    n = lax.axis_size("seq")
    vmem = pl.BlockSpec(memory_space=pltpu.VMEM)
    hbm = pl.BlockSpec(memory_space=pltpu.HBM)
    V = pltpu.VMEM
    dma = pltpu.SemaphoreType.DMA
    return pl.pallas_call(
        functools.partial(kernel, n, groups, heads),
        out_shape=jax.ShapeDtypeStruct((tokens, width), BF16),
        in_specs=[hbm] * 9,
        out_specs=vmem,
        scratch_shapes=[
            V((chunks, tokens, wide), BF16),
            V((tokens, groups * 2 * state), BF16),
            V((chunks, tokens, wide), BF16),
            V((heads, tokens), F32),
            V(conv_x.shape, F32),
            V(conv_bc.shape, F32),
            V((1, heads), F32),
            pltpu.SMEM((heads,), F32),
            V((1, width), F32),
            V((HALO, width), BF16),
            V((HALO, groups * 2 * state), BF16),
            V((chunks, state, wide), BF16),
            V((chunks, state, wide), BF16),
            V((chunks, state, wide), F32),
            V((chunks, tokens, wide), F32),
            V((chunks, tokens, wide), F32),
            V((tokens + 8, wide), F32),
            V((tokens + 8, groups * 2 * state), F32),
            V((chunks, tokens, wide), BF16),
            V((heads, tokens), F32),
            V((heads, tokens), F32),
            V((chunks, tokens, per_chunk), F32),
            V((chunks, tokens, per_chunk), F32),
            V((128, tokens), F32),
            V((tokens, 128), F32),
            V((groups, tokens, tokens), F32),
            V((groups, tokens, state), BF16),
            V((groups, state, tokens), BF16),
            dma((2,)),
            dma((2,)),
            dma((chunks,)),
            dma((chunks,)),
            dma((chunks,)),
            dma((chunks,)),
            dma((7,)),
        ],
        compiler_params=pltpu.CompilerParams(
            collective_id=0, has_side_effects=True, vmem_limit_bytes=LIMIT
        ),
    )(
        x_in, bc_in.reshape(tokens, groups * 2 * state), z_in, dt_raw.T, conv_x, conv_bc,
        a_log.reshape(1, heads), d_skip, norm_gain.reshape(1, width),
    )


def solution(mesh):
    return jax.shard_map(
        shards,
        mesh=mesh,
        in_specs=(
            P(("groups", "seq"), "head"),
            P(("groups", "seq"), "head", None),
            P(("groups", "seq"), "head"),
            P(("groups", "seq"), "head"),
            P(None, "head"),
            P(None, "head", None),
            P("head"),
            P("head"),
            P("head"),
        ),
        out_specs=P(("groups", "seq"), "head"),
        check_vma=False,
    )
```

```python
import functools

import jax
import jax.numpy as jnp
from jax import lax
from jax.experimental import pallas as pl
from jax.experimental.pallas import tpu as pltpu
from jax.sharding import PartitionSpec as P

BLOCK = 128
EPS = 1e-05
HALO = 16
LIMIT = 55000000
HEADS_PER_CHUNK = 4
F32 = jnp.float32
BF16 = jnp.bfloat16
MESH = pl.DeviceIdType.MESH


def silu(v):
    half = 0.5 * v
    return half + half * jnp.tanh(half)


def kernel(
    n, groups, heads, x_hbm, bc_hbm, z_hbm, dt_hbm, cx_hbm, cbc_hbm, al_hbm, ds_hbm, gain_hbm,
    o_ref, x_ref, bc_ref, z_ref, dt_ref, cx_ref, cbc_ref, al_ref, ds_ref, gain_ref, xh, bh, sendb, recvb, own, gated, ec, xs, bs, xact, cum_t, dt_t, col_cum, col_tail,
    pad, square, inter, c_act, b_t, h_send, h_recv, s_send, s_recv, x_sem, z_sem, p_sem,
):
    tokens, width = x_hbm.shape
    head_dim = width // heads
    per_chunk = xact.shape[2] // head_dim
    wide = xact.shape[2]
    chunks = width // wide
    group_chunks = chunks // groups
    state = bc_hbm.shape[1] // groups // 2
    taps = cx_ref.shape[0]
    base = 8 - (taps - 1)
    me = lax.axis_index("seq")

    def halo_copies():
        rows = pl.ds(tokens - HALO, HALO)
        return [
            pltpu.make_async_remote_copy(
                src_ref=src.at[rows], dst_ref=dst, send_sem=h_send.at[i], recv_sem=h_recv.at[i],
                device_id={"seq": me + 1}, device_id_type=MESH,
            )
            for i, (src, dst) in enumerate(((bc_hbm, bh), (x_hbm, xh)))
        ]

    def state_copy(k):
        return pltpu.make_async_remote_copy(
            src_ref=sendb.at[k], dst_ref=recvb.at[k], send_sem=s_send.at[k],
            recv_sem=s_recv.at[k], device_id={"seq": me + 1}, device_id_type=MESH,
        )

    def columns_of(k):
        return pl.ds(pl.multiple_of(k * wide, wide), wide)

    def x_copy(k):
        return pltpu.make_async_copy(x_hbm.at[:, columns_of(k)], x_ref.at[k], x_sem.at[k])

    def z_copy(k):
        return pltpu.make_async_copy(z_hbm.at[:, columns_of(k)], z_ref.at[k], z_sem.at[k])

    pairs = (
        (dt_hbm, dt_ref), (al_hbm, al_ref), (cbc_hbm, cbc_ref), (cx_hbm, cx_ref),
        (ds_hbm, ds_ref), (gain_hbm, gain_ref), (bc_hbm, bc_ref),
    )
    small = [pltpu.make_async_copy(a, b, p_sem.at[i]) for i, (a, b) in enumerate(pairs)]

    barrier = pltpu.get_barrier_semaphore()

    @pl.when(me > 0)
    def _():
        pl.semaphore_signal(barrier, inc=1, device_id={"seq": me - 1}, device_id_type=MESH)

    for copy in small:
        copy.start()

    def fetch_x(k, carry):
        x_copy(k).start()
        return carry

    def fetch_z(k, carry):
        z_copy(k).start()
        return carry

    lax.fori_loop(0, chunks, fetch_x, 0)

    @pl.when(me < n - 1)
    def _():
        pl.semaphore_wait(barrier, 1)
        for copy in halo_copies():
            copy.start()

    row = lax.broadcasted_iota(jnp.int32, (tokens, tokens), 0)
    col = lax.broadcasted_iota(jnp.int32, (tokens, tokens), 1)
    causal = row >= col
    small[0].wait()
    small[1].wait()
    raw = dt_ref[...]
    softplus = jnp.maximum(raw, 0.0) + jnp.log1p(jnp.exp(-jnp.abs(raw)))
    dt_t[...] = softplus
    pad[...] = jnp.zeros_like(pad)
    pad[:heads] = softplus
    deltas = pad[...].T[:, :heads]
    rates = -jnp.exp(al_ref[...]) * deltas
    cum = jnp.dot(
        causal.astype(F32), rates, precision=lax.Precision.HIGHEST, preferred_element_type=F32
    )
    tail = jnp.exp(cum[tokens - 1 : tokens] - cum) * deltas
    for k in range(chunks):
        part = slice(k * per_chunk, (k + 1) * per_chunk)
        col_cum[k] = cum[:, part]
        col_tail[k] = tail[:, part]
    square[...] = jnp.zeros_like(square)
    square[:, :heads] = cum
    cum_t[...] = square[...].T[:heads]

    lax.fori_loop(0, chunks, fetch_z, 0)

    @pl.when(me == 0)
    def _():
        xh[...] = jnp.zeros_like(xh)
        bh[...] = jnp.zeros_like(bh)

    @pl.when(me > 0)
    def _():
        for copy in halo_copies():
            copy.wait_recv()

    small[2].wait()
    small[6].wait()
    bs[0:8] = bh[...].astype(F32)[HALO - 8 :]
    bs[8:] = bc_ref[...].astype(F32)
    for g in range(groups):
        span = slice(g * 2 * state, (g + 1) * 2 * state)
        total = cbc_ref[0, g : g + 1, :] * bs[base : base + tokens, span]
        for k in range(1, taps):
            total = total + cbc_ref[k, g : g + 1, :] * bs[base + k : base + k + tokens, span]
        act = silu(total)
        b_part = act[:, :state].astype(BF16)
        c_part = act[:, state:].astype(BF16)
        c_act[g] = c_part
        b_t[g] = b_part.astype(F32).T.astype(BF16)
        product = lax.dot_general(
            c_part, b_part, (((1,), (1,)), ((), ())), preferred_element_type=F32
        )
        inter[g] = jnp.where(causal, product, 0.0)

    head_of_lane = lax.broadcasted_iota(jnp.int32, (tokens, wide), 1) // head_dim

    def spread(columns):
        result = jnp.broadcast_to(columns[:, per_chunk - 1 :], (tokens, wide))
        for h in range(per_chunk - 2, -1, -1):
            result = jnp.where(head_of_lane == h, columns[:, h : h + 1], result)
        return result

    for copy in small[3:6]:
        copy.wait()

    def make_state(g, k):
        cols = columns_of(k)
        x_copy(k).wait()
        xs[0:8] = xh[:, cols].astype(F32)[HALO - 8 :]
        xs[8:] = x_ref[k].astype(F32)
        weights = cx_ref[:, cols]
        total = weights[0:1] * xs[base : base + tokens]
        for i in range(1, taps):
            total = total + weights[i : i + 1] * xs[base + i : base + i + tokens]
        act = silu(total).astype(BF16)
        xact[k] = act
        ec[k] = jnp.exp(spread(col_cum[k]))
        scaled = (spread(col_tail[k]) * act.astype(F32)).astype(BF16)
        made = jnp.dot(b_t[g], scaled, preferred_element_type=F32)
        own[k] = made

        @pl.when((me == 0) & (me < n - 1))
        def _():
            sendb[k] = made.astype(BF16)
            state_copy(k).start()


    def group_step(g, carry):
        def chunk_step(j, squares):
            k = g * group_chunks + j
            make_state(g, k)

            @pl.when(me > 0)
            def _():
                state_copy(k).wait_recv()

            @pl.when((me > 0) & (me < n - 1))
            def _():
                decay = ec[k, tokens - 1 : tokens, :]
                sendb[k] = (decay * recvb[k].astype(F32) + own[k]).astype(BF16)
                state_copy(k).start()

            act = xact[k]
            columns = col_cum[k]
            parts = []
            skips = jnp.zeros((1, wide), F32)
            for h in range(per_chunk):
                at = k * per_chunk + h
                gap = jnp.minimum(columns[:, h : h + 1] - cum_t[pl.ds(at, 1), :], 0.0)
                weight = (jnp.exp(gap) * dt_t[pl.ds(at, 1), :] * inter[g]).astype(BF16)
                parts.append(
                    jnp.dot(
                        weight, act[:, h * head_dim : (h + 1) * head_dim],
                        preferred_element_type=F32,
                    )
                )
                skips = jnp.where(head_of_lane[0:1] == h, ds_ref[at], skips)
            gated[k] = jnp.concatenate(parts, axis=1) + skips * act.astype(F32)

            z_copy(k).wait()
            gate = silu(z_ref[k].astype(F32))

            @pl.when(me > 0)
            def _():
                gated[k] += ec[k] * jnp.dot(c_act[g], recvb[k], preferred_element_type=F32)

            done = gated[k] * gate
            gated[k] = done
            return squares + jnp.sum(done * done, axis=1, keepdims=True)

        squares = lax.fori_loop(0, group_chunks, chunk_step, jnp.zeros((tokens, 1), F32))
        scale = lax.rsqrt(squares * (groups / width) + EPS)

        def finish(j, carry):
            k = g * group_chunks + j
            cols = columns_of(k)
            o_ref[:, cols] = (gated[k] * scale * gain_ref[:, cols]).astype(BF16)
            return carry

        return lax.fori_loop(0, group_chunks, finish, carry)

    lax.fori_loop(0, groups, group_step, 0)

    @pl.when(me < n - 1)
    def _():
        for copy in halo_copies():
            copy.wait_send()

        def drain(k, carry):
            state_copy(k).wait_send()
            return carry

        lax.fori_loop(0, chunks, drain, 0)


def shards(x_in, bc_in, z_in, dt_raw, conv_x, conv_bc, a_log, d_skip, norm_gain):
    tokens, width = x_in.shape
    assert tokens == BLOCK
    groups = bc_in.shape[1]
    heads = dt_raw.shape[1]
    state = bc_in.shape[2] // 2
    head_dim = width // heads
    per_chunk = min(HEADS_PER_CHUNK, heads // groups)
    wide = per_chunk * head_dim
    chunks = width // wide
    n = lax.axis_size("seq")
    vmem = pl.BlockSpec(memory_space=pltpu.VMEM)
    hbm = pl.BlockSpec(memory_space=pltpu.HBM)
    V = pltpu.VMEM
    dma = pltpu.SemaphoreType.DMA
    return pl.pallas_call(
        functools.partial(kernel, n, groups, heads),
        out_shape=jax.ShapeDtypeStruct((tokens, width), BF16),
        in_specs=[hbm] * 9,
        out_specs=vmem,
        scratch_shapes=[
            V((chunks, tokens, wide), BF16),
            V((tokens, groups * 2 * state), BF16),
            V((chunks, tokens, wide), BF16),
            V((heads, tokens), F32),
            V(conv_x.shape, F32),
            V(conv_bc.shape, F32),
            V((1, heads), F32),
            pltpu.SMEM((heads,), F32),
            V((1, width), F32),
            V((HALO, width), BF16),
            V((HALO, groups * 2 * state), BF16),
            V((chunks, state, wide), BF16),
            V((chunks, state, wide), BF16),
            V((chunks, state, wide), F32),
            V((chunks, tokens, wide), F32),
            V((chunks, tokens, wide), F32),
            V((tokens + 8, wide), F32),
            V((tokens + 8, groups * 2 * state), F32),
            V((chunks, tokens, wide), BF16),
            V((heads, tokens), F32),
            V((heads, tokens), F32),
            V((chunks, tokens, per_chunk), F32),
            V((chunks, tokens, per_chunk), F32),
            V((128, tokens), F32),
            V((tokens, 128), F32),
            V((groups, tokens, tokens), F32),
            V((groups, tokens, state), BF16),
            V((groups, state, tokens), BF16),
            dma((2,)),
            dma((2,)),
            dma((chunks,)),
            dma((chunks,)),
            dma((chunks,)),
            dma((chunks,)),
            dma((7,)),
        ],
        compiler_params=pltpu.CompilerParams(
            collective_id=0, has_side_effects=True, vmem_limit_bytes=LIMIT
        ),
    )(
        x_in, bc_in.reshape(tokens, groups * 2 * state), z_in, dt_raw.T, conv_x, conv_bc,
        a_log.reshape(1, heads), d_skip, norm_gain.reshape(1, width),
    )


def solution(mesh):
    return jax.shard_map(
        shards,
        mesh=mesh,
        in_specs=(
            P(("groups", "seq"), "head"),
            P(("groups", "seq"), "head", None),
            P(("groups", "seq"), "head"),
            P(("groups", "seq"), "head"),
            P(None, "head"),
            P(None, "head", None),
            P("head"),
            P("head"),
            P("head"),
        ),
        out_specs=P(("groups", "seq"), "head"),
        check_vma=False,
    )
```
